256 devices in a mesh: seq: 64 (over y, z, core), head: 4 (over x).
Axes of the slice: x: 4, y: 4, z: 8, core: 2. Of those that a mesh axis runs over, the one named last changes fastest.
Arguments:
- x_loader: bfloat16 [16384, 2048], P('seq', 'head'), may hold values from -6 to 6
- dest: int32 [16384], P('seq'), may hold values from 0 to 16383, as said below
- doc_start: int32 [16384], P('seq'), may hold values from 0 to 16383, as said below
- w_qk: bfloat16 [2048, 2, 2048], P(None, None, 'head'), may hold values from -0.125 to 0.125
- w_v: bfloat16 [2048, 2048], P(None, 'head'), may hold values from -0.125 to 0.125
- w_beta: bfloat16 [2048, 16], P(None, 'head'), may hold values from -0.125 to 0.125
- beta_bias: float32 [16], P('head'), may hold values from -6 to 3
- out_gain: float32 [128], replicated, may hold values from 0.25 to 1.75
Outputs:
- mixed_heads: bfloat16 [16384, 2048], P('seq', 'head')
The draws below stay inside these ranges and needn't reach their ends.
Inputs may be any that keep to these rules, and one draw needn't show every extreme that they name: dest is a permutation of the positions; the 256 rows of each aligned loader block hold exactly 4 positions of every aligned block of 256 positions. doc_start[p] is the first position of p's document: it never falls along the positions, equals p where a document begins, and positions 0 and 16383 each begin a document; there are at most 32 documents.
All inputs are finite; a program needn't handle non-finite values.
Results may differ from the reference program's by a relative error of at most 0.0055.
Values may be sent and summed in bfloat16 or wider, within the bound.
No kernel may reach another device: no remote copies, remote signals or barrier semaphores. Data moves between devices by JAX's collectives and lax.ppermute only.
A program may use at most 64 MiB of HBM per device.

```python
import jax
import jax.numpy as jnp
from jax import lax

D = 2048
H = 16
DK = 128
DV = 128
SPAN = 64
TOK_DEV = 256
TOKENS = 16384
PER_PEER = 4
DOCS = 32


def shuffle_one(subkey):
    return jax.random.permutation(subkey, TOK_DEV)


def draw_dest(key, part):
    shard_count = TOKENS // TOK_DEV
    keys_dest = jax.random.split(jax.random.fold_in(key, 17), shard_count)
    keys_source = jax.random.split(jax.random.fold_in(key, 29), shard_count)
    dealt = jax.vmap(shuffle_one)(keys_dest)
    shuffled = jax.vmap(shuffle_one)(keys_source)
    source_shard = dealt // PER_PEER
    within = dealt % PER_PEER
    dest_shard = jnp.arange(shard_count, dtype=jnp.int32)[:, None]
    loader_row = source_shard * TOK_DEV + shuffled[source_shard, dest_shard * PER_PEER + within]
    position = dest_shard * TOK_DEV + jnp.arange(TOK_DEV, dtype=jnp.int32)[None, :]
    return jnp.zeros((TOKENS,), jnp.int32).at[loader_row.reshape(-1)].set(position.reshape(-1).astype(jnp.int32))


def draw_doc_start(key, part):
    upper = max(TOKENS // 4, 2)
    inner = jax.random.randint(jax.random.fold_in(key, 41), (DOCS - 2,), 1, upper).astype(jnp.int32)
    marks = jnp.zeros((TOKENS,), jnp.int32).at[inner].set(inner)
    marks = marks.at[TOKENS - 1].set(TOKENS - 1)
    return lax.cummax(marks, axis=0)


def shard_levels(rng, shape, pieces, smallest, largest):
    gain, own = 1.0, jax.random.fold_in(rng, 6)
    for dim, parts in pieces:
        draws = jnp.exp(jax.random.uniform(jax.random.fold_in(own, dim), (parts,), jnp.float32, smallest / len(pieces), largest / len(pieces)))
        gain = gain * jnp.repeat(draws, shape[dim] // parts).reshape([-1 if axis == dim else 1 for axis in range(len(shape))])
    return gain


def gaussian(stream_key, dims, spread, most, shards=(), kind=jnp.bfloat16):
    values = spread * jax.random.normal(stream_key, dims, jnp.float32)
    if shards:
        values = values * shard_levels(stream_key, dims, shards, -0.22, 0.18)
    return jnp.clip(values, -most, most).astype(kind)


def setup_inputs(seed: int = 0) -> dict:
    streams_of = jax.random.split(jax.random.key(seed), 9)
    return {
        "x_loader": gaussian(streams_of[0], (TOKENS, D), 1.0, 6.0, ((0, 64), (1, 4))),
        "dest": draw_dest(jax.random.fold_in(streams_of[8], 71), 0),
        "doc_start": draw_doc_start(jax.random.fold_in(streams_of[8], 71), 0),
        "w_qk": gaussian(streams_of[3], (D, 2, H * DK), D ** -0.5, 0.125, ((2, 4),)),
        "w_v": gaussian(streams_of[4], (D, H * DV), D ** -0.5, 0.125, ((1, 4),)),
        "w_beta": gaussian(streams_of[5], (D, H), D ** -0.5, 0.125, ((1, 4),)),
        "beta_bias": jnp.clip(-6.0 + 9.0 * jax.random.uniform(streams_of[6], (H,), jnp.float32) ** shard_levels(streams_of[6], (H,), ((0, 4),), -0.2, 0.2), -6.0, 3.0),
        "out_gain": jnp.clip(1.0 + 0.15 * jax.random.normal(streams_of[7], (DV,), jnp.float32), 0.25, 1.75),
    }


beta_limit = 0.1
key_eps = 1e-06
rms_eps = 1e-05
highest = lax.Precision.HIGHEST

def activate(qk_raw, value_raw, beta_logit, beta_bias, head_count):
    count_rows = qk_raw.shape[0]
    width_key = qk_raw.shape[1] // (2 * head_count)
    width_value = value_raw.shape[1] // head_count
    queries = jax.nn.silu(qk_raw[:, :head_count * width_key].astype(jnp.float32)).reshape(count_rows, head_count, width_key)
    keys_raw = jax.nn.silu(qk_raw[:, head_count * width_key:].astype(jnp.float32)).reshape(count_rows, head_count, width_key)
    keys_unit = keys_raw / jnp.sqrt(lax.optimization_barrier(jnp.sum(keys_raw * keys_raw, axis=-1, keepdims=True)) + key_eps)
    values = jax.nn.silu(value_raw.astype(jnp.float32)).reshape(count_rows, head_count, width_value)
    beta_rate = beta_limit * jax.nn.sigmoid(beta_logit + beta_bias)
    return (queries, keys_unit, values, beta_rate)

def to_blocks(array, block_len):
    return array.reshape(array.shape[0] // block_len, block_len, array.shape[1], array.shape[2]).transpose(0, 2, 1, 3)

def block_terms(queries, keys_unit, values, beta_rate, doc_ids, starts):
    block_len = doc_ids.shape[-1]
    position = jnp.arange(block_len)
    same_doc = doc_ids[:, :, None] == doc_ids[:, None, :]
    strict_mask = (same_doc & (position[:, None] > position[None, :])).astype(jnp.float32)
    incl_mask = (same_doc & (position[:, None] >= position[None, :])).astype(jnp.float32)
    carried = (doc_ids < starts[:, None]).astype(jnp.float32)
    last_doc = (doc_ids == doc_ids[:, -1:]).astype(jnp.float32)
    gram_keys = jnp.einsum('nhid,nhjd->nhij', keys_unit, keys_unit, precision=highest) * strict_mask[:, None]
    nilpotent = beta_rate[..., :, None] * gram_keys
    identity = jnp.eye(block_len, dtype=jnp.float32)
    power_term = nilpotent
    inverse = identity - nilpotent
    for factor in range(block_len.bit_length() - 2):
        power_term = jnp.einsum('nhij,nhjk->nhik', power_term, power_term, precision=highest)
        inverse = jnp.einsum('nhij,nhjk->nhik', inverse, identity + power_term, precision=highest)
    weighted = inverse * beta_rate[..., None, :]
    fresh = jnp.einsum('nhij,nhje->nhie', weighted, values, precision=highest)
    correction = jnp.einsum('nhij,nhjd->nhid', weighted, keys_unit * carried[:, None, :, None], precision=highest)
    scores = jnp.einsum('nhid,nhjd->nhij', queries, keys_unit, precision=highest) * incl_mask[:, None]
    local_out = jnp.einsum('nhij,nhje->nhie', scores, fresh, precision=highest)
    query_state = queries * carried[:, None, :, None] - jnp.einsum('nhij,nhjd->nhid', scores, correction, precision=highest)
    last_keys = keys_unit * last_doc[:, None, :, None]
    width_key = keys_unit.shape[-1]
    transition = carried[:, -1][:, None, None, None] * jnp.eye(width_key, dtype=jnp.float32) - jnp.einsum('nhcd,nhce->nhde', last_keys, correction, precision=highest)
    offset = jnp.einsum('nhcd,nhce->nhde', last_keys, fresh, precision=highest)
    return (local_out, query_state, transition, offset)

def finish(outputs, out_gain):
    mean_square = lax.optimization_barrier(jnp.mean(outputs * outputs, axis=-1, keepdims=True))
    scaled = outputs * lax.rsqrt(mean_square + rms_eps) * out_gain
    return scaled.reshape(outputs.shape[0], -1).astype(jnp.bfloat16)

def reference(x_loader, dest, doc_start, w_qk, w_v, w_beta, beta_bias, out_gain):
    packed = jnp.zeros((TOKENS, D), jnp.bfloat16).at[dest].set(x_loader)
    qk_raw = jnp.dot(packed, w_qk.reshape(D, 2 * H * DK), preferred_element_type=jnp.float32).astype(jnp.bfloat16)
    value_raw = jnp.dot(packed, w_v, preferred_element_type=jnp.float32).astype(jnp.bfloat16)
    beta_logit = jnp.dot(packed, w_beta, preferred_element_type=jnp.float32)
    queries, keys_unit, values, beta_rate = activate(qk_raw, value_raw, beta_logit, beta_bias, H)
    block_count = TOKENS // SPAN
    inputs_all = (to_blocks(queries, SPAN), to_blocks(keys_unit, SPAN), to_blocks(values, SPAN), beta_rate.reshape(block_count, SPAN, H).transpose(0, 2, 1), doc_start.reshape(block_count, SPAN), jnp.arange(block_count, dtype=jnp.int32) * SPAN)

    def advance(state_now, inputs):
        q_block, k_block, v_block, b_block, d_block, s_block = inputs
        local_out, query_state, transition, offset = block_terms(q_block[None], k_block[None], v_block[None], b_block[None], d_block[None], s_block[None])
        result = local_out[0] + jnp.einsum('hcd,hde->hce', query_state[0], state_now, precision=highest)
        state_next = jnp.einsum('hde,hef->hdf', transition[0], state_now, precision=highest) + offset[0]
        return (state_next, result)
    initial = jnp.zeros((H, DK, DV), jnp.float32)
    final_state, block_out = lax.scan(advance, initial, inputs_all)
    outputs = block_out.transpose(0, 2, 1, 3).reshape(TOKENS, H, DV)
    return finish(outputs, out_gain)
```

```python
import jax
import jax.numpy as jnp
from jax import lax
from jax.experimental import pallas as pl
from jax.experimental.pallas import tpu as pltpu
from jax.sharding import Mesh
from jax.sharding import PartitionSpec as P


SEQ = ("y", "zh", "zl", "c")
NEAR = ("zl", "c")
ROWS = 256
HALF = 128
WIDE = 512
HEADS = 4
KEY = 128
beta_limit = 0.1
key_eps = 1e-06
rms_eps = 1e-05
bf16 = jnp.bfloat16
f32 = jnp.float32
ANY = pl.BlockSpec(memory_space=pl.ANY)
VM = pl.BlockSpec(memory_space=pltpu.VMEM)


def mm(a, b):
    return lax.dot_general(a, b, (((1,), (0,)), ((), ())), preferred_element_type=f32)


def mm_nt(a, b):
    return lax.dot_general(a, b, (((1,), (1,)), ((), ())), preferred_element_type=f32)


def mm_tn(a, b):
    return lax.dot_general(a, b, (((0,), (0,)), ((), ())), preferred_element_type=f32)


def iotas(n):
    return (
        lax.broadcasted_iota(jnp.int32, (n, n), 0),
        lax.broadcasted_iota(jnp.int32, (n, n), 1),
    )


def call(kernel, outs, scratch, args, specs=None, flops=0, moved=0):
    return pl.pallas_call(
        kernel,
        out_shape=outs,
        in_specs=specs or [VM] * len(args),
        out_specs=[VM] * len(outs),
        scratch_shapes=scratch,
        cost_estimate=pl.CostEstimate(flops=flops, bytes_accessed=moved, transcendentals=0),
        compiler_params=pltpu.CompilerParams(vmem_limit_bytes=48 * 2**20),
    )(*args)


def order_kernel(dest_ref, x_ref, out_ref):
    dest = dest_ref[...].astype(f32)
    across = jnp.broadcast_to(dest, (ROWS, ROWS))
    down = across.T
    rank = jnp.sum((down < across).astype(f32), axis=0, keepdims=True)
    row, _ = iotas(ROWS)
    pick = (rank == row.astype(f32)).astype(bf16)
    moved = mm(pick, x_ref[...]).astype(bf16)
    place = jnp.sum(pick.astype(f32) * (dest_ref[...] & (ROWS - 1)).astype(f32), axis=1, keepdims=True)
    place = jnp.broadcast_to(place, (ROWS, KEY)).astype(bf16)
    peers, per_peer = out_ref.shape[:2]
    for s in range(peers):
        out_ref[s, :, :WIDE] = moved[s * per_peer : (s + 1) * per_peer]
        out_ref[s, :, WIDE:] = place[s * per_peer : (s + 1) * per_peer]


def place_kernel(got_ref, out_ref, rows):
    peers, per_peer = got_ref.shape[:2]
    for s in range(peers):
        rows[s * per_peer : (s + 1) * per_peer, :] = got_ref[s]
    place = rows[:, WIDE:].astype(f32).T[:1]
    slot, _ = iotas(ROWS)
    pick = (place == slot.astype(f32)).astype(bf16)
    out_ref[...] = mm(pick, rows[:, :WIDE]).astype(bf16)


def silu(a):
    return a / (1.0 + jnp.exp(-a))


def doc_masks(doc_ref, t0):
    across = jnp.broadcast_to(doc_ref[...].astype(f32), (ROWS, ROWS))
    down = across.T
    same = across == down
    col = down[:, :1]
    carried = (col < t0).astype(f32)
    last = (col == col[ROWS - 1 : ROWS]).astype(f32)
    return same, carried, last


def first_row():
    return (lax.axis_index(SEQ) * ROWS).astype(f32)


def near_index():
    return lax.axis_index("zl") * 2 + lax.axis_index("c")


def terms_kernel(
    x0, x1, x3, x2a, x2b, wqk_hbm, wv_hbm, wb_ref, bias_ref, doc_ref,
    m0, m1, m2, m3, q_out, k_out, y_out,
    wqk, wv, acc, maps, sems,
):
    me = lax.axis_index("head")
    blocks = ((x0, 0), (x1, 3), (x3, 1), (None, 2))
    copies = []
    for n, (_, off) in enumerate(blocks):
        start = pl.multiple_of(lax.rem(me + off, 4) * WIDE, WIDE)
        a = pltpu.make_async_copy(wqk_hbm.at[pl.ds(start, WIDE)], wqk.at[n], sems.at[n, 0])
        b = pltpu.make_async_copy(wv_hbm.at[pl.ds(start, WIDE)], wv.at[n], sems.at[n, 1])
        a.start()
        b.start()
        copies.append((a, b, start))
    logit = None
    for n, (ref, _) in enumerate(blocks):
        a, b, start = copies[n]
        x = ref[...] if ref is not None else jnp.concatenate([x2a[...], x2b[...]], axis=0)
        part = mm_nt(x, wb_ref[:, pl.ds(start, WIDE)])
        logit = part if logit is None else logit + part
        a.wait()
        b.wait()
        for t in range(6):
            w = wqk[n, :, t * 256 : t * 256 + 256] if t < 4 else wv[n, :, t * 256 - 1024 : t * 256 - 768]
            part = mm(x, w)
            if n == 0:
                acc[:, t * 256 : t * 256 + 256] = part
            else:
                acc[:, t * 256 : t * 256 + 256] += part
    beta_all = beta_limit * (1.0 / (1.0 + jnp.exp(-(logit + bias_ref[...]))))

    same, carried, last = doc_masks(doc_ref, first_row())
    row, col = iotas(ROWS)
    strict = same & (row > col)
    r, c = iotas(HALF)
    eye = (r == c).astype(f32)
    by16 = (r >> 4) == (c >> 4)

    def level(s):
        return ((r >> (s + 1)) == (c >> (s + 1))) & ((r >> s) != (c >> s))

    rhs, cross, low = [], [], []
    for h in range(HEADS):
        def raw(base):
            piece = acc[:, base + h * KEY : base + (h + 1) * KEY]
            return silu(piece.astype(bf16).astype(f32))

        q_out[h] = raw(0).astype(bf16)
        k = raw(WIDE)
        k = k / jnp.sqrt(jnp.sum(k * k, axis=-1, keepdims=True) + key_eps)
        kb = k.astype(bf16)
        k_out[h] = kb
        v = raw(2 * WIDE)
        beta = beta_all[:, h : h + 1]
        rhs.append(jnp.concatenate([(beta * carried) * k, beta * v], axis=1).astype(bf16))
        top, bot = kb[:HALF], kb[HALF:]
        b_top, b_bot = beta[:HALF], beta[HALF:]
        low.append(jnp.where(strict[:HALF, :HALF], b_top * mm_nt(top, top), 0.0))
        low.append(jnp.where(strict[HALF:, HALF:], b_bot * mm_nt(bot, bot), 0.0))
        cross.append(jnp.where(strict[HALF:, :HALF], b_bot * mm_nt(bot, top), 0.0).astype(bf16))

    n1 = [jnp.where(by16, m, 0.0) for m in low]
    inv = [eye - m for m in n1]
    power = [m.astype(bf16) for m in n1]
    for _ in range(3):
        power = [mm(m, m).astype(bf16) for m in power]
        inv = [x + mm(x.astype(bf16), m) for x, m in zip(inv, power)]
    for s in (4, 5, 6):
        mask = level(s)
        xb = [x.astype(bf16) for x in inv]
        mid = [mm(jnp.where(mask, m, 0.0).astype(bf16), x).astype(bf16) for m, x in zip(low, xb)]
        inv = [x - mm(y, m) for x, y, m in zip(inv, xb, mid)]
    inv = [x.astype(bf16) for x in inv]
    y_top = [mm(inv[2 * h], rhs[h][:HALF]).astype(bf16) for h in range(HEADS)]
    y_mid = [(rhs[h][HALF:].astype(f32) - mm(cross[h], y_top[h])).astype(bf16) for h in range(HEADS)]
    y_bot = [mm(inv[2 * h + 1], y_mid[h]).astype(bf16) for h in range(HEADS)]
    reset = jnp.where(carried[ROWS - 1 : ROWS] > 0, 0.0, 1.0) * eye
    reset = jnp.concatenate([reset, jnp.zeros((KEY, KEY), f32)], axis=1)
    for h in range(HEADS):
        y_out[h, :HALF] = y_top[h]
        y_out[h, HALF:] = y_bot[h]
        last_keys = (k_out[h].astype(f32) * last).astype(bf16)
        total = mm_tn(last_keys[:HALF], y_top[h]) + mm_tn(last_keys[HALF:], y_bot[h])
        maps[h] = (total + reset).astype(bf16)
    near = near_index()
    for n, ref in enumerate((m0, m1, m2, m3)):
        ref[...] = maps[lax.rem(near + n, 4)]


def read_kernel(q_ref, k_ref, y_ref, doc_ref, local_out, query_out):
    same, carried, _ = doc_masks(doc_ref, first_row())
    row, col = iotas(ROWS)
    mask = same & (row >= col)
    for h in range(HEADS):
        scores = jnp.where(mask, mm_nt(q_ref[h], k_ref[h]), 0.0).astype(bf16)
        both = mm(scores, y_ref[h])
        query_out[h] = (q_ref[h].astype(f32) * carried - both[:, :KEY]).astype(bf16)
        local_out[h] = both[:, KEY:]


def after(first, then):
    firm = first.astype(bf16)
    return firm.astype(f32) + then.astype(f32) - mm(then[:, :KEY].astype(bf16), firm)


def chosen(which, options):
    out = options[0]
    for n in range(1, len(options)):
        out = jnp.where(which == n, options[n], out)
    return out


def in_order(me, refs, slots):
    for n, ref in enumerate(refs):
        slots[lax.rem(me + 4 - n, 4)] = ref[...]


def near_kernel(a, b, c, d, total, prefix, slots):
    in_order(near_index(), (a, b, c, d), slots)
    run = slots[0]
    prefix[0] = run
    for n in (1, 2, 3):
        run = after(run, slots[n]).astype(bf16)
        if n < 3:
            prefix[n] = run
    total[...] = run


def far_kernel(a, b, c, d, total, prefix, slots):
    me = lax.axis_index("zh")
    in_order(me, (a, b, c, d), slots)
    run = slots[0].astype(f32)
    seen = [jnp.zeros_like(run), run]
    for n in (1, 2, 3):
        run = after(run, slots[n])
        seen.append(run)
    total[...] = run.astype(bf16)
    prefix[...] = chosen(me, seen[:4]).astype(bf16)


def apply_map(step, state):
    firm = state.astype(bf16)
    return firm.astype(f32) - mm(step[:, :KEY], firm) + step[:, KEY:].astype(f32)


def state_kernel(a, b, c, d, far, near, s0, s1, s2, s3, slots, states):
    me = lax.axis_index("y")
    in_order(me, (a, b, c, d), slots)
    state = jnp.zeros((KEY, KEY), f32)
    seen = [state]
    for n in range(3):
        state = slots[n][:, KEY:].astype(f32) if n == 0 else apply_map(slots[n], state)
        seen.append(state)
    group = apply_map(far[...], chosen(me, seen)).astype(bf16)
    states[0] = group
    for n in range(3):
        states[n + 1] = apply_map(near[n], group).astype(bf16)
    place = near_index()
    for n, ref in enumerate((s0, s1, s2, s3)):
        ref[...] = states[lax.rem(place + n, 4)]


def out_kernel(a, b, c, d, local_ref, query_ref, gain_ref, out_ref, slots):
    in_order(near_index(), (a, b, c, d), slots)
    for h in range(HEADS):
        out = local_ref[h] + mm(query_ref[h], slots[h])
        mean = jnp.mean(out * out, axis=-1, keepdims=True)
        out_ref[:, h * KEY : (h + 1) * KEY] = (out * lax.rsqrt(mean + rms_eps) * gain_ref[...]).astype(bf16)


def turned(x, axis, by):
    return lax.ppermute(x, axis, [(i, (i + by) % 4) for i in range(4)])


def local(x_loader, dest, doc_start, w_qk, w_v, w_beta, beta_bias, out_gain):
    shape = jax.ShapeDtypeStruct
    peers = lax.axis_size(SEQ)
    vmem = pltpu.VMEM
    doc = doc_start.reshape(1, ROWS)
    (sent,) = call(
        order_kernel, [shape((peers, ROWS // peers, WIDE + KEY), bf16)], [], (dest.reshape(1, ROWS), x_loader)
    )
    got = lax.all_to_all(sent, SEQ, split_axis=0, concat_axis=0, tiled=True)
    (packed,) = call(place_kernel, [shape((ROWS, WIDE), bf16)], [vmem((ROWS, WIDE + KEY), bf16)], (got,))
    from_left = turned(packed, "head", 1)
    from_right = turned(packed, "head", 3)
    across_a = turned(packed[:HALF], "head", 2)
    across_b = turned(packed[HALF:], "head", 2)
    flat_qk = w_qk.reshape(w_qk.shape[0], -1)
    one_map = shape((KEY, 2 * KEY), bf16)
    args = (
        packed, from_left, from_right, across_a, across_b,
        flat_qk, w_v, w_beta.T, beta_bias.reshape(1, HEADS), doc,
    )
    m0, m1, m2, m3, q, k, y = call(
        terms_kernel,
        [one_map] * 4
        + [shape((HEADS, ROWS, KEY), bf16), shape((HEADS, ROWS, KEY), bf16), shape((HEADS, ROWS, 2 * KEY), bf16)],
        [
            vmem((4, WIDE, 2 * WIDE), bf16),
            vmem((4, WIDE, WIDE), bf16),
            vmem((ROWS, 3 * WIDE), f32),
            vmem((HEADS, KEY, 2 * KEY), bf16),
            pltpu.SemaphoreType.DMA((4, 2)),
        ],
        args,
        specs=[VM] * 5 + [ANY] * 2 + [VM] * 3,
        flops=4 * 10**9,
        moved=8 * 10**6,
    )
    slots = [vmem((4, KEY, 2 * KEY), bf16)]
    near = (m0, turned(m1, NEAR, 1), turned(m2, NEAR, 2), turned(m3, NEAR, 3))
    local_out, query = call(
        read_kernel,
        [shape((HEADS, ROWS, KEY), f32), shape((HEADS, ROWS, KEY), bf16)],
        [],
        (q, k, y, doc),
        flops=10**9,
        moved=2 * 10**6,
    )
    group, prefix = call(near_kernel, [one_map, shape((3, KEY, 2 * KEY), bf16)], slots, near)
    far = (group, *(turned(group, "zh", n) for n in (1, 2, 3)))
    plane, far_prefix = call(far_kernel, [one_map, one_map], slots, far)
    planes = (plane, *(turned(plane, "y", n) for n in (1, 2, 3)))
    s0, s1, s2, s3 = call(
        state_kernel,
        [shape((KEY, KEY), bf16)] * 4,
        slots + [vmem((4, KEY, KEY), bf16)],
        (*planes, far_prefix, prefix),
    )
    states = (s0, turned(s1, NEAR, 1), turned(s2, NEAR, 2), turned(s3, NEAR, 3))
    (out,) = call(
        out_kernel,
        [shape((ROWS, WIDE), bf16)],
        [vmem((4, KEY, KEY), bf16)],
        (*states, local_out, query, out_gain.reshape(1, KEY)),
    )
    return out


def solution(mesh):
    torus = Mesh(mesh.devices.reshape(4, 4, 2, 2, mesh.shape["head"]), (*SEQ, "head"))
    return jax.shard_map(
        local,
        mesh=torus,
        in_specs=(
            P(SEQ, "head"),
            P(SEQ),
            P(SEQ),
            P(None, None, "head"),
            P(None, "head"),
            P(None, "head"),
            P("head"),
            P(),
        ),
        out_specs=P(SEQ, "head"),
        check_vma=False,
    )
```

```python
import jax
import jax.numpy as jnp
from jax import lax
from jax.experimental import pallas as pl
from jax.experimental.pallas import tpu as pltpu
from jax.sharding import Mesh
from jax.sharding import PartitionSpec as P


SEQ = ("y", "zh", "zl", "c")
NEAR = ("zl", "c")
CHIPS = ("y", "zh", "zl")
ROWS = 256
HALF = 128
WIDE = 512
HEADS = 4
KEY = 128
beta_limit = 0.1
key_eps = 1e-06
rms_eps = 1e-05
bf16 = jnp.bfloat16
f32 = jnp.float32
ANY = pl.BlockSpec(memory_space=pl.ANY)
VM = pl.BlockSpec(memory_space=pltpu.VMEM)


def mm(a, b):
    return lax.dot_general(a, b, (((1,), (0,)), ((), ())), preferred_element_type=f32)


def mm_nt(a, b):
    return lax.dot_general(a, b, (((1,), (1,)), ((), ())), preferred_element_type=f32)


def mm_tn(a, b):
    return lax.dot_general(a, b, (((0,), (0,)), ((), ())), preferred_element_type=f32)


def iotas(n):
    return (
        lax.broadcasted_iota(jnp.int32, (n, n), 0),
        lax.broadcasted_iota(jnp.int32, (n, n), 1),
    )


def call(kernel, outs, scratch, args, specs=None, flops=0, moved=0):
    return pl.pallas_call(
        kernel,
        out_shape=outs,
        in_specs=specs or [VM] * len(args),
        out_specs=[VM] * len(outs),
        scratch_shapes=scratch,
        cost_estimate=pl.CostEstimate(flops=flops, bytes_accessed=moved, transcendentals=0),
        compiler_params=pltpu.CompilerParams(vmem_limit_bytes=24 * 2**20),
    )(*args)


def order_kernel(dest_hbm, x_hbm, keep_ref, send_ref, dest_ref, x_ref, sems):
    first = pltpu.make_async_copy(dest_hbm, dest_ref, sems.at[0])
    second = pltpu.make_async_copy(x_hbm, x_ref, sems.at[1])
    first.start()
    second.start()
    mine = lax.axis_index("c")
    row, _ = iotas(ROWS)
    core = jnp.where(row < HALF, mine, 1 - mine)
    wanted = (((row & (HALF - 1)) >> 2) * 8 + core * 4 + (row & 3)).astype(f32)
    first.wait()
    dest = dest_ref[...].astype(f32)
    across = jnp.broadcast_to(dest, (ROWS, ROWS))
    down = across.T
    rank = jnp.sum((down < across).astype(f32), axis=0, keepdims=True)
    pick = (rank == wanted).astype(bf16)
    place = jnp.sum(pick.astype(f32) * (dest_ref[...] & (ROWS - 1)).astype(f32), axis=1, keepdims=True)
    place = jnp.broadcast_to(place, (ROWS, KEY)).astype(bf16)
    second.wait()
    moved = mm(pick, x_ref[...]).astype(bf16)
    for n, ref in enumerate((keep_ref, send_ref)):
        for s in range(ref.shape[0]):
            rows = slice(n * HALF + 4 * s, n * HALF + 4 * s + 4)
            ref[s, :, :WIDE] = moved[rows]
            ref[s, :, WIDE:] = place[rows]


def merge_kernel(keep_ref, got_ref, out_ref):
    out_ref[:, :, : WIDE + KEY] = keep_ref[...]
    out_ref[:, :, WIDE + KEY :] = got_ref[...]


def place_kernel(got_ref, out_ref, rows):
    for s in range(got_ref.shape[0]):
        for n in range(2):
            rows[8 * s + 4 * n : 8 * s + 4 * n + 4, :] = got_ref[s, :, n * (WIDE + KEY) : (n + 1) * (WIDE + KEY)]
    place = rows[:, WIDE:].astype(f32).T[:1]
    slot, _ = iotas(ROWS)
    pick = (place == slot.astype(f32)).astype(bf16)
    out_ref[...] = mm(pick, rows[:, :WIDE]).astype(bf16)


def silu(a):
    return a / (1.0 + jnp.exp(-a))


def doc_masks(doc_ref, t0):
    across = jnp.broadcast_to(doc_ref[...].astype(f32), (ROWS, ROWS))
    down = across.T
    same = across == down
    col = down[:, :1]
    carried = (col < t0).astype(f32)
    last = (col == col[ROWS - 1 : ROWS]).astype(f32)
    return same, carried, last


def first_row():
    return (lax.axis_index(SEQ) * ROWS).astype(f32)


def near_index():
    return lax.axis_index("zl") * 2 + lax.axis_index("c")


def project(pairs, wqk, wv, wb, acc, logit):
    for n, (x, off) in enumerate(pairs):
        start = pl.multiple_of(lax.rem(lax.axis_index("head") + off, 4) * WIDE, WIDE)
        part = mm_nt(x, wb[:, pl.ds(start, WIDE)])
        logit = part if logit is None else logit + part
        pairs[n] = (x, start)
    tiles = []
    for t in range(6):
        cols = slice(t * 256, t * 256 + 256)
        total = None if acc is None else acc[:, cols]
        for x, start in pairs:
            w = wqk[pl.ds(start, WIDE), cols] if t < 4 else wv[pl.ds(start, WIDE), t * 256 - 1024 : t * 256 - 768]
            part = mm(x, w)
            total = part if total is None else total + part
        tiles.append(total)
    return tiles, logit


def own_kernel(x0, wqk, wv, wb, acc_out, logit_out):
    tiles, logit_out[...] = project([(x0[...], 0)], wqk, wv, wb, None, None)
    for t in range(6):
        acc_out[:, t * 256 : t * 256 + 256] = tiles[t]


def beside_kernel(x1, x3, wqk, wv, wb, acc_in, logit_in, acc_out, logit_out):
    tiles, logit_out[...] = project([(x1[...], 3), (x3[...], 1)], wqk, wv, wb, acc_in, logit_in[...])
    for t in range(6):
        acc_out[:, t * 256 : t * 256 + 256] = tiles[t]


def terms_kernel(
    x2, wqk, wv, wb, acc_in, logit_in, bias_ref, doc_ref,
    m0, m1, m2, m3, q_out, k_out, y_out,
    acc, maps,
):
    tiles, logit = project([(x2[...], 2)], wqk, wv, wb, acc_in, logit_in[...])
    for t in range(6):
        acc[:, t * 256 : t * 256 + 256] = tiles[t]
    beta_all = beta_limit * (1.0 / (1.0 + jnp.exp(-(logit + bias_ref[...]))))

    same, carried, last = doc_masks(doc_ref, first_row())
    row, col = iotas(ROWS)
    strict = same & (row > col)
    r, c = iotas(HALF)
    eye = (r == c).astype(f32)
    by16 = (r >> 4) == (c >> 4)

    def level(s):
        return ((r >> (s + 1)) == (c >> (s + 1))) & ((r >> s) != (c >> s))

    rhs, cross, low = [], [], []
    for h in range(HEADS):
        def raw(base):
            piece = acc[:, base + h * KEY : base + (h + 1) * KEY]
            return silu(piece.astype(bf16).astype(f32))

        q_out[h] = raw(0).astype(bf16)
        k = raw(WIDE)
        k = k / jnp.sqrt(jnp.sum(k * k, axis=-1, keepdims=True) + key_eps)
        kb = k.astype(bf16)
        k_out[h] = kb
        v = raw(2 * WIDE)
        beta = beta_all[:, h : h + 1]
        rhs.append(jnp.concatenate([(beta * carried) * k, beta * v], axis=1).astype(bf16))
        top, bot = kb[:HALF], kb[HALF:]
        b_top, b_bot = beta[:HALF], beta[HALF:]
        low.append(jnp.where(strict[:HALF, :HALF], b_top * mm_nt(top, top), 0.0))
        low.append(jnp.where(strict[HALF:, HALF:], b_bot * mm_nt(bot, bot), 0.0))
        cross.append(jnp.where(strict[HALF:, :HALF], b_bot * mm_nt(bot, top), 0.0).astype(bf16))

    n1 = [jnp.where(by16, m, 0.0) for m in low]
    inv = [eye - m for m in n1]
    power = [m.astype(bf16) for m in n1]
    for _ in range(3):
        power = [mm(m, m).astype(bf16) for m in power]
        inv = [x + mm(x.astype(bf16), m) for x, m in zip(inv, power)]
    for s in (4, 5, 6):
        mask = level(s)
        xb = [x.astype(bf16) for x in inv]
        mid = [mm(jnp.where(mask, m, 0.0).astype(bf16), x).astype(bf16) for m, x in zip(low, xb)]
        inv = [x - mm(y, m) for x, y, m in zip(inv, xb, mid)]
    inv = [x.astype(bf16) for x in inv]
    y_top = [mm(inv[2 * h], rhs[h][:HALF]).astype(bf16) for h in range(HEADS)]
    y_mid = [(rhs[h][HALF:].astype(f32) - mm(cross[h], y_top[h])).astype(bf16) for h in range(HEADS)]
    y_bot = [mm(inv[2 * h + 1], y_mid[h]).astype(bf16) for h in range(HEADS)]
    reset = jnp.where(carried[ROWS - 1 : ROWS] > 0, 0.0, 1.0) * eye
    reset = jnp.concatenate([reset, jnp.zeros((KEY, KEY), f32)], axis=1)
    for h in range(HEADS):
        y_out[h, :HALF] = y_top[h]
        y_out[h, HALF:] = y_bot[h]
        last_keys = (k_out[h].astype(f32) * last).astype(bf16)
        total = mm_tn(last_keys[:HALF], y_top[h]) + mm_tn(last_keys[HALF:], y_bot[h])
        maps[h] = (total + reset).astype(bf16)
    near = near_index()
    for n, ref in enumerate((m0, m1, m2, m3)):
        ref[...] = maps[near ^ n]


def read_kernel(q_ref, k_ref, y_ref, doc_ref, local_out, query_out):
    same, carried, _ = doc_masks(doc_ref, first_row())
    row, col = iotas(ROWS)
    mask = same & (row >= col)
    for h in range(HEADS):
        scores = jnp.where(mask, mm_nt(q_ref[h], k_ref[h]), 0.0).astype(bf16)
        both = mm(scores, y_ref[h])
        query_out[h] = (q_ref[h].astype(f32) * carried - both[:, :KEY]).astype(bf16)
        local_out[h] = both[:, KEY:]


def after(first, then):
    firm = first.astype(bf16)
    return firm.astype(f32) + then.astype(f32) - mm(then[:, :KEY].astype(bf16), firm)


def chosen(which, options):
    out = options[0]
    for n in range(1, len(options)):
        out = jnp.where(which == n, options[n], out)
    return out


def in_order(me, refs, slots):
    for n, ref in enumerate(refs):
        slots[me ^ n] = ref[...]


def near_kernel(a, b, c, d, total, prefix, slots):
    in_order(near_index(), (a, b, c, d), slots)
    run = slots[0]
    prefix[0] = run
    for n in (1, 2, 3):
        run = after(run, slots[n]).astype(bf16)
        if n < 3:
            prefix[n] = run
    total[...] = run


def pair_kernel(mine, other, total, first_out):
    upper = (lax.axis_index("zh") & 1) == 1
    first = jnp.where(upper, other[...], mine[...])
    total[...] = after(first, jnp.where(upper, mine[...], other[...])).astype(bf16)
    first_out[...] = first


def far_kernel(mine, other, first, total, prefix):
    me = lax.axis_index("zh")
    upper = me >= 2
    low = jnp.where(upper, other[...], mine[...])
    total[...] = after(low, jnp.where(upper, mine[...], other[...])).astype(bf16)
    low = low.astype(f32)
    later = after(low, first[...])
    prefix[...] = chosen(me, [jnp.zeros_like(low), first[...].astype(f32), low, later]).astype(bf16)


def apply_map(step, state):
    firm = state.astype(bf16)
    return firm.astype(f32) - mm(step[:, :KEY], firm) + step[:, KEY:].astype(f32)


def state_kernel(a, b, c, d, far, near, s0, s1, s2, s3, slots, states):
    me = lax.axis_index("y")
    in_order(me, (a, b, c, d), slots)
    state = jnp.zeros((KEY, KEY), f32)
    seen = [state]
    for n in range(3):
        state = slots[n][:, KEY:].astype(f32) if n == 0 else apply_map(slots[n], state)
        seen.append(state)
    group = apply_map(far[...], chosen(me, seen)).astype(bf16)
    states[0] = group
    for n in range(3):
        states[n + 1] = apply_map(near[n], group).astype(bf16)
    place = near_index()
    for n, ref in enumerate((s0, s1, s2, s3)):
        ref[...] = states[place ^ n]


def out_kernel(a, b, c, d, local_ref, query_ref, gain_ref, out_ref, slots):
    in_order(near_index(), (a, b, c, d), slots)
    for h in range(HEADS):
        out = local_ref[h] + mm(query_ref[h], slots[h])
        mean = jnp.mean(out * out, axis=-1, keepdims=True)
        out_ref[:, h * KEY : (h + 1) * KEY] = (out * lax.rsqrt(mean + rms_eps) * gain_ref[...]).astype(bf16)


def turned(x, axis, by):
    return lax.ppermute(x, axis, [(i, (i + by) % 4) for i in range(4)])


def swapped(x, axis, by):
    return lax.ppermute(x, axis, [(i, i ^ by) for i in range(4)])


def local(x_loader, dest, doc_start, w_qk, w_v, w_beta, beta_bias, out_gain):
    shape = jax.ShapeDtypeStruct
    vmem = pltpu.VMEM
    doc = doc_start.reshape(1, ROWS)
    chips = lax.axis_size(CHIPS)
    half = shape((chips, 4, WIDE + KEY), bf16)
    keep, send = call(
        order_kernel,
        [half, half],
        [vmem((1, ROWS), jnp.int32), vmem((ROWS, WIDE), bf16), pltpu.SemaphoreType.DMA((2,))],
        (dest.reshape(1, ROWS), x_loader),
        specs=[ANY, ANY],
    )
    got = lax.ppermute(send, "c", [(0, 1), (1, 0)])
    (sent,) = call(merge_kernel, [shape((chips, 4, 2 * (WIDE + KEY)), bf16)], [], (keep, got))
    got = lax.all_to_all(sent, CHIPS, split_axis=0, concat_axis=0, tiled=True)
    flat_qk = w_qk.reshape(w_qk.shape[0], -1)
    (packed,) = call(place_kernel, [shape((ROWS, WIDE), bf16)], [vmem((ROWS, WIDE + KEY), bf16)], (got,))
    from_left = turned(packed, "head", 1)
    from_right = turned(packed, "head", 3)
    across = turned(packed, "head", 2)
    weights = (flat_qk, w_v, w_beta.T)
    sums = [shape((ROWS, 3 * WIDE), f32), shape((ROWS, HEADS), f32)]
    part = call(own_kernel, sums, [], (packed, *weights), flops=4 * 10**8, moved=3 * 10**6)
    part = call(
        beside_kernel, sums, [], (from_left, from_right, *weights, *part), flops=8 * 10**8, moved=6 * 10**6
    )
    one_map = shape((KEY, 2 * KEY), bf16)
    m0, m1, m2, m3, q, k, y = call(
        terms_kernel,
        [one_map] * 4
        + [shape((HEADS, ROWS, KEY), bf16), shape((HEADS, ROWS, KEY), bf16), shape((HEADS, ROWS, 2 * KEY), bf16)],
        [vmem((ROWS, 3 * WIDE), f32), vmem((HEADS, KEY, 2 * KEY), bf16)],
        (across, *weights, *part, beta_bias.reshape(1, HEADS), doc),
        flops=2 * 10**9,
        moved=4 * 10**6,
    )
    slots = [vmem((4, KEY, 2 * KEY), bf16)]
    n3, n2, n1 = (swapped(m, NEAR, n) for m, n in ((m3, 3), (m2, 2), (m1, 1)))
    near = (m0, n1, n2, n3)
    local_out, query = call(
        read_kernel,
        [shape((HEADS, ROWS, KEY), f32), shape((HEADS, ROWS, KEY), bf16)],
        [],
        (q, k, y, doc),
        flops=10**9,
        moved=2 * 10**6,
    )
    group, prefix = call(near_kernel, [one_map, shape((3, KEY, 2 * KEY), bf16)], slots, near)
    half_plane, first = call(pair_kernel, [one_map, one_map], [], (group, swapped(group, "zh", 1)))
    plane, far_prefix = call(
        far_kernel, [one_map, one_map], [], (half_plane, swapped(half_plane, "zh", 3), first)
    )
    p1, p3, p2 = (swapped(plane, "y", n) for n in (1, 3, 2))
    planes = (plane, p1, p2, p3)
    s0, s1, s2, s3 = call(
        state_kernel,
        [shape((KEY, KEY), bf16)] * 4,
        slots + [vmem((4, KEY, KEY), bf16)],
        (*planes, far_prefix, prefix),
    )
    t3, t2, t1 = (swapped(m, NEAR, n) for m, n in ((s3, 3), (s2, 2), (s1, 1)))
    states = (s0, t1, t2, t3)
    (out,) = call(
        out_kernel,
        [shape((ROWS, WIDE), bf16)],
        [vmem((4, KEY, KEY), bf16)],
        (*states, local_out, query, out_gain.reshape(1, KEY)),
    )
    return out


def solution(mesh):
    torus = Mesh(mesh.devices.reshape(4, 4, 2, 2, mesh.shape["head"]), (*SEQ, "head"))
    return jax.shard_map(
        local,
        mesh=torus,
        in_specs=(
            P(SEQ, "head"),
            P(SEQ),
            P(SEQ),
            P(None, None, "head"),
            P(None, "head"),
            P(None, "head"),
            P("head"),
            P(),
        ),
        out_specs=P(SEQ, "head"),
        check_vma=False,
    )
```

```python
import jax
import jax.numpy as jnp
from jax import lax
from jax.experimental import pallas as pl
from jax.experimental.pallas import tpu as pltpu
from jax.sharding import Mesh
from jax.sharding import PartitionSpec as P


SEQ = ("y", "zh", "zl", "c")
NEAR = ("zl", "c")
ROWS = 256
HALF = 128
WIDE = 512
HEADS = 4
KEY = 128
beta_limit = 0.1
key_eps = 1e-06
rms_eps = 1e-05
bf16 = jnp.bfloat16
f32 = jnp.float32
ANY = pl.BlockSpec(memory_space=pl.ANY)
VM = pl.BlockSpec(memory_space=pltpu.VMEM)


def mm(a, b):
    return lax.dot_general(a, b, (((1,), (0,)), ((), ())), preferred_element_type=f32)


def mm_nt(a, b):
    return lax.dot_general(a, b, (((1,), (1,)), ((), ())), preferred_element_type=f32)


def mm_tn(a, b):
    return lax.dot_general(a, b, (((0,), (0,)), ((), ())), preferred_element_type=f32)


def iotas(n):
    return (
        lax.broadcasted_iota(jnp.int32, (n, n), 0),
        lax.broadcasted_iota(jnp.int32, (n, n), 1),
    )


def call(kernel, outs, scratch, args, specs=None, flops=0, moved=0, into=VM):
    return pl.pallas_call(
        kernel,
        out_shape=outs,
        in_specs=specs or [VM] * len(args),
        out_specs=[into] * len(outs),
        scratch_shapes=scratch,
        cost_estimate=pl.CostEstimate(flops=flops, bytes_accessed=moved, transcendentals=0),
        compiler_params=pltpu.CompilerParams(vmem_limit_bytes=24 * 2**20),
    )(*args)


def order_kernel(dest_hbm, x_hbm, out_ref, dest_ref, x_ref, sems):
    first = pltpu.make_async_copy(dest_hbm, dest_ref, sems.at[0])
    second = pltpu.make_async_copy(x_hbm, x_ref, sems.at[1])
    first.start()
    second.start()
    row, _ = iotas(ROWS)
    first.wait()
    dest = dest_ref[...].astype(f32)
    across = jnp.broadcast_to(dest, (ROWS, ROWS))
    down = across.T
    rank = jnp.sum((down < across).astype(f32), axis=0, keepdims=True)
    pick = (rank == row.astype(f32)).astype(bf16)
    place = jnp.sum(pick.astype(f32) * (dest_ref[...] & (ROWS - 1)).astype(f32), axis=1, keepdims=True)
    place = jnp.broadcast_to(place, (ROWS, KEY)).astype(bf16)
    second.wait()
    moved = mm(pick, x_ref[...]).astype(bf16)
    for s in range(out_ref.shape[0]):
        for n in range(2):
            pair = slice(4 * s + 2 * n, 4 * s + 2 * n + 2)
            out_ref[s, :, n * WIDE : (n + 1) * WIDE] = moved[pair]
            out_ref[s, :, 2 * WIDE + n * 64 : 2 * WIDE + n * 64 + 64] = place[pair, n * 64 : n * 64 + 64]


def place_kernel(got_ref, weights_ref, upper_ref, lower_ref, low, high, places):
    for s in range(got_ref.shape[0]):
        pair = slice(2 * s, 2 * s + 2)
        low[pair, :] = got_ref[s, :, :WIDE]
        high[pair, :] = got_ref[s, :, WIDE : 2 * WIDE]
        places[pair, :] = got_ref[s, :, 2 * WIDE :]
    place = places[...].astype(f32).T
    slot = lax.broadcasted_iota(jnp.int32, (ROWS, HALF), 0).astype(f32)
    out = mm((place[:1] == slot).astype(bf16), low[...]) + mm((place[64:65] == slot).astype(bf16), high[...])
    upper_ref[...] = out[:HALF].astype(bf16)
    lower_ref[...] = out[HALF:].astype(bf16)


def silu(a):
    return a / (1.0 + jnp.exp(-a))


def doc_masks(doc_ref, t0):
    across = jnp.broadcast_to(doc_ref[...].astype(f32), (ROWS, ROWS))
    down = across.T
    same = across == down
    col = down[:, :1]
    carried = (col < t0).astype(f32)
    last = (col == col[ROWS - 1 : ROWS]).astype(f32)
    return same, carried, last


def first_row():
    return (lax.axis_index(SEQ) * ROWS).astype(f32)


def near_index():
    return lax.axis_index("zl") * 2 + lax.axis_index("c")


def project(pairs, wqk, wv, wb, acc, logit):
    for n, (x, off) in enumerate(pairs):
        start = pl.multiple_of(lax.rem(lax.axis_index("head") + off, 4) * WIDE, WIDE)
        part = mm_nt(x, wb[:, pl.ds(start, WIDE)])
        logit = part if logit is None else logit + part
        pairs[n] = (x, start)
    tiles = []
    for t in range(6):
        cols = slice(t * 256, t * 256 + 256)
        total = None if acc is None else acc[:, cols]
        for x, start in pairs:
            w = wqk[pl.ds(start, WIDE), cols] if t < 4 else wv[pl.ds(start, WIDE), t * 256 - 1024 : t * 256 - 768]
            part = mm(x, w)
            total = part if total is None else total + part
        tiles.append(total)
    return tiles, logit


def both(a, b):
    return jnp.concatenate([a[...], b[...]], axis=0)


def own_kernel(x0a, x0b, wqk, wv, wb, acc_out, logit_out):
    tiles, logit_out[...] = project([(both(x0a, x0b), 0)], wqk, wv, wb, None, None)
    for t in range(6):
        acc_out[:, t * 256 : t * 256 + 256] = tiles[t]


def beside_kernel(x1a, x1b, x3a, x3b, wqk, wv, wb, acc_in, logit_in, acc_out, logit_out):
    tiles, logit_out[...] = project([(both(x1a, x1b), 3), (both(x3a, x3b), 1)], wqk, wv, wb, acc_in, logit_in[...])
    for t in range(6):
        acc_out[:, t * 256 : t * 256 + 256] = tiles[t]


def terms_kernel(
    x2a, x2b, wqk, wv, wb, acc_in, logit_in, bias_ref, doc_ref,
    m0, m1, m2, m3, q_out, k_out, y_out,
    acc, maps,
):
    tiles, logit = project([(both(x2a, x2b), 2)], wqk, wv, wb, acc_in, logit_in[...])
    for t in range(6):
        acc[:, t * 256 : t * 256 + 256] = tiles[t]
    beta_all = beta_limit * (1.0 / (1.0 + jnp.exp(-(logit + bias_ref[...]))))

    same, carried, last = doc_masks(doc_ref, first_row())
    row, col = iotas(ROWS)
    strict = same & (row > col)
    r, c = iotas(HALF)
    eye = (r == c).astype(f32)
    by16 = (r >> 4) == (c >> 4)

    def level(s):
        return ((r >> (s + 1)) == (c >> (s + 1))) & ((r >> s) != (c >> s))

    q_out[...] = acc[:, :WIDE].astype(bf16)
    rhs, cross, low = [], [], []
    for h in range(HEADS):
        def raw(base):
            piece = acc[:, base + h * KEY : base + (h + 1) * KEY]
            return silu(piece.astype(bf16).astype(f32))

        k = raw(WIDE)
        k = k / jnp.sqrt(jnp.sum(k * k, axis=-1, keepdims=True) + key_eps)
        kb = k.astype(bf16)
        k_out[h] = kb
        v = raw(2 * WIDE)
        beta = beta_all[:, h : h + 1]
        rhs.append(jnp.concatenate([(beta * carried) * k, beta * v], axis=1).astype(bf16))
        top, bot = kb[:HALF], kb[HALF:]
        b_top, b_bot = beta[:HALF], beta[HALF:]
        low.append(jnp.where(strict[:HALF, :HALF], b_top * mm_nt(top, top), 0.0))
        low.append(jnp.where(strict[HALF:, HALF:], b_bot * mm_nt(bot, bot), 0.0))
        cross.append(jnp.where(strict[HALF:, :HALF], b_bot * mm_nt(bot, top), 0.0).astype(bf16))

    n1 = [jnp.where(by16, m, 0.0) for m in low]
    inv = [eye - m for m in n1]
    power = [m.astype(bf16) for m in n1]
    for _ in range(3):
        power = [mm(m, m).astype(bf16) for m in power]
        inv = [x + mm(x.astype(bf16), m) for x, m in zip(inv, power)]
    for s in (4, 5, 6):
        mask = level(s)
        xb = [x.astype(bf16) for x in inv]
        mid = [mm(jnp.where(mask, m, 0.0).astype(bf16), x).astype(bf16) for m, x in zip(low, xb)]
        inv = [x - mm(y, m) for x, y, m in zip(inv, xb, mid)]
    inv = [x.astype(bf16) for x in inv]
    y_top = [mm(inv[2 * h], rhs[h][:HALF]).astype(bf16) for h in range(HEADS)]
    y_mid = [(rhs[h][HALF:].astype(f32) - mm(cross[h], y_top[h])).astype(bf16) for h in range(HEADS)]
    y_bot = [mm(inv[2 * h + 1], y_mid[h]).astype(bf16) for h in range(HEADS)]
    reset = jnp.where(carried[ROWS - 1 : ROWS] > 0, 0.0, 1.0) * eye
    reset = jnp.concatenate([reset, jnp.zeros((KEY, KEY), f32)], axis=1)
    for h in range(HEADS):
        y_out[h, :HALF] = y_top[h]
        y_out[h, HALF:] = y_bot[h]
        last_keys = (k_out[h].astype(f32) * last).astype(bf16)
        total = mm_tn(last_keys[:HALF], y_top[h]) + mm_tn(last_keys[HALF:], y_bot[h])
        maps[h] = (total + reset).astype(bf16)
    near = near_index()
    for n, ref in enumerate((m0, m1, m2, m3)):
        ref[...] = maps[near ^ n]


def read_kernel(q_ref, k_ref, y_ref, doc_ref, local_out, query_out):
    same, carried, _ = doc_masks(doc_ref, first_row())
    row, col = iotas(ROWS)
    mask = same & (row >= col)
    for h in range(HEADS):
        q = silu(q_ref[:, h * KEY : (h + 1) * KEY].astype(f32))
        scores = jnp.where(mask, mm_nt(q.astype(bf16), k_ref[h]), 0.0).astype(bf16)
        both = mm(scores, y_ref[h])
        query_out[h] = (q * carried - both[:, :KEY]).astype(bf16)
        local_out[h] = both[:, KEY:]


def after(first, then):
    firm = first.astype(bf16)
    return firm.astype(f32) + then.astype(f32) - mm(then[:, :KEY].astype(bf16), firm)


def chosen(which, options):
    out = options[0]
    for n in range(1, len(options)):
        out = jnp.where(which == n, options[n], out)
    return out


def in_order(me, refs, slots):
    for n, ref in enumerate(refs):
        slots[me ^ n] = ref[...]


def near_kernel(a, b, c, d, total, prefix, slots):
    in_order(near_index(), (a, b, c, d), slots)
    run = slots[0]
    prefix[0] = run
    for n in (1, 2, 3):
        run = after(run, slots[n]).astype(bf16)
        if n < 3:
            prefix[n] = run
    total[...] = run


def pair_kernel(mine, other, total, first_out):
    upper = (lax.axis_index("zh") & 1) == 1
    first = jnp.where(upper, other[...], mine[...])
    total[...] = after(first, jnp.where(upper, mine[...], other[...])).astype(bf16)
    first_out[...] = first


def far_kernel(mine, other, first, total, prefix):
    me = lax.axis_index("zh")
    upper = me >= 2
    low = jnp.where(upper, other[...], mine[...])
    total[...] = after(low, jnp.where(upper, mine[...], other[...])).astype(bf16)
    low = low.astype(f32)
    later = after(low, first[...])
    prefix[...] = chosen(me, [jnp.zeros_like(low), first[...].astype(f32), low, later]).astype(bf16)


def apply_map(step, state):
    firm = state.astype(bf16)
    return firm.astype(f32) - mm(step[:, :KEY], firm) + step[:, KEY:].astype(f32)


def state_kernel(a, b, c, d, far, near, s0, s1, s2, s3, slots, states):
    me = lax.axis_index("y")
    in_order(me, (a, b, c, d), slots)
    state = jnp.zeros((KEY, KEY), f32)
    seen = [state]
    for n in range(3):
        state = slots[n][:, KEY:].astype(f32) if n == 0 else apply_map(slots[n], state)
        seen.append(state)
    group = apply_map(far[...], chosen(me, seen)).astype(bf16)
    states[0] = group
    for n in range(3):
        states[n + 1] = apply_map(near[n], group).astype(bf16)
    place = near_index()
    for n, ref in enumerate((s0, s1, s2, s3)):
        ref[...] = states[place ^ n]


def out_kernel(a, b, c, d, local_ref, query_ref, gain_ref, out_hbm, slots, done, sems):
    in_order(near_index(), (a, b, c, d), slots)
    copies = []
    for h in range(HEADS):
        out = local_ref[h] + mm(query_ref[h], slots[h])
        mean = jnp.mean(out * out, axis=-1, keepdims=True)
        done[h] = (out * lax.rsqrt(mean + rms_eps) * gain_ref[...]).astype(bf16)
        copies.append(pltpu.make_async_copy(done.at[h], out_hbm.at[:, pl.ds(h * KEY, KEY)], sems.at[h]))
        copies[h].start()
    for copy in copies:
        copy.wait()


def turned(x, axis, by):
    return lax.ppermute(x, axis, [(i, (i + by) % 4) for i in range(4)])


def swapped(x, axis, by):
    return lax.ppermute(x, axis, [(i, i ^ by) for i in range(4)])


def local(x_loader, dest, doc_start, w_qk, w_v, w_beta, beta_bias, out_gain):
    shape = jax.ShapeDtypeStruct
    vmem = pltpu.VMEM
    doc = doc_start.reshape(1, ROWS)
    peers = lax.axis_size(SEQ)
    in_hbm = pl.BlockSpec(memory_space=pltpu.HBM)
    (sent,) = call(
        order_kernel,
        [shape((peers, 2, 2 * WIDE + KEY), bf16)],
        [vmem((1, ROWS), jnp.int32), vmem((ROWS, WIDE), bf16), pltpu.SemaphoreType.DMA((2,))],
        [pltpu.with_memory_space_constraint(x, pltpu.HBM) for x in (dest.reshape(1, ROWS), x_loader)],
        specs=[in_hbm, in_hbm],
    )
    got = lax.all_to_all(sent, SEQ, split_axis=0, concat_axis=0, tiled=True)
    flat_qk = w_qk.reshape(w_qk.shape[0], -1)
    upper, lower = call(place_kernel, [shape((HALF, WIDE), bf16)] * 2, [vmem((HALF, WIDE), bf16), vmem((HALF, WIDE), bf16), vmem((HALF, KEY), bf16)], (got, pltpu.with_memory_space_constraint(flat_qk, pltpu.HBM)), specs=[VM, in_hbm])
    left_upper = turned(upper, "head", 1)
    right_lower = turned(lower, "head", 3)
    left_lower = turned(lower, "head", 1)
    right_upper = turned(upper, "head", 3)
    across_upper = turned(left_upper, "head", 1)
    across_lower = turned(right_lower, "head", 3)
    weights = (flat_qk, w_v, w_beta.T)
    sums = [shape((ROWS, 3 * WIDE), f32), shape((ROWS, HEADS), f32)]
    part = call(own_kernel, sums, [], (upper, lower, *weights), flops=4 * 10**8, moved=3 * 10**6)
    part = call(
        beside_kernel, sums, [], (left_upper, left_lower, right_upper, right_lower, *weights, *part), flops=8 * 10**8, moved=6 * 10**6
    )
    one_map = shape((KEY, 2 * KEY), bf16)
    m0, m1, m2, m3, q, k, y = call(
        terms_kernel,
        [one_map] * 4
        + [shape((ROWS, WIDE), bf16), shape((HEADS, ROWS, KEY), bf16), shape((HEADS, ROWS, 2 * KEY), bf16)],
        [vmem((ROWS, 3 * WIDE), f32), vmem((HEADS, KEY, 2 * KEY), bf16)],
        (across_upper, across_lower, *weights, *part, beta_bias.reshape(1, HEADS), doc),
        flops=2 * 10**9,
        moved=4 * 10**6,
    )
    slots = [vmem((4, KEY, 2 * KEY), bf16)]
    n3, n2, n1 = (swapped(m, NEAR, n) for m, n in ((m3, 3), (m2, 2), (m1, 1)))
    near = (m0, n1, n2, n3)
    local_out, query = call(
        read_kernel,
        [shape((HEADS, ROWS, KEY), f32), shape((HEADS, ROWS, KEY), bf16)],
        [],
        (q, k, y, doc),
        flops=10**9,
        moved=2 * 10**6,
    )
    group, prefix = call(near_kernel, [one_map, shape((3, KEY, 2 * KEY), bf16)], slots, near)
    half_plane, first = call(pair_kernel, [one_map, one_map], [], (group, swapped(group, "zh", 1)))
    plane, far_prefix = call(
        far_kernel, [one_map, one_map], [], (half_plane, swapped(half_plane, "zh", 3), first)
    )
    p1, p3, p2 = (swapped(plane, "y", n) for n in (1, 3, 2))
    planes = (plane, p1, p2, p3)
    s0, s1, s2, s3 = call(
        state_kernel,
        [shape((KEY, KEY), bf16)] * 4,
        slots + [vmem((4, KEY, KEY), bf16)],
        (*planes, far_prefix, prefix),
    )
    t3, t2, t1 = (swapped(m, NEAR, n) for m, n in ((s3, 3), (s2, 2), (s1, 1)))
    states = (s0, t1, t2, t3)
    (out,) = call(
        out_kernel,
        [shape((ROWS, WIDE), bf16)],
        [vmem((4, KEY, KEY), bf16), vmem((HEADS, ROWS, KEY), bf16), pltpu.SemaphoreType.DMA((HEADS,))],
        (*states, local_out, query, out_gain.reshape(1, KEY)),
        into=ANY,
    )
    return out


def solution(mesh):
    torus = Mesh(mesh.devices.reshape(4, 4, 2, 2, mesh.shape["head"]), (*SEQ, "head"))
    return jax.shard_map(
        local,
        mesh=torus,
        in_specs=(
            P(SEQ, "head"),
            P(SEQ),
            P(SEQ),
            P(None, None, "head"),
            P(None, "head"),
            P(None, "head"),
            P("head"),
            P(),
        ),
        out_specs=P(SEQ, "head"),
        check_vma=False,
    )
```

```python
import jax
import jax.numpy as jnp
from jax import lax
from jax.experimental import pallas as pl
from jax.experimental.pallas import tpu as pltpu
from jax.sharding import Mesh
from jax.sharding import PartitionSpec as P


SEQ = ("y", "zh", "zl", "c")
NEAR = ("zl", "c")
ROWS = 256
HALF = 128
WIDE = 512
HEADS = 4
KEY = 128
beta_limit = 0.1
key_eps = 1e-06
rms_eps = 1e-05
bf16 = jnp.bfloat16
f32 = jnp.float32
ANY = pl.BlockSpec(memory_space=pl.ANY)
VM = pl.BlockSpec(memory_space=pltpu.VMEM)


def mm(a, b):
    return lax.dot_general(a, b, (((1,), (0,)), ((), ())), preferred_element_type=f32)


def mm_nt(a, b):
    return lax.dot_general(a, b, (((1,), (1,)), ((), ())), preferred_element_type=f32)


def mm_tn(a, b):
    return lax.dot_general(a, b, (((0,), (0,)), ((), ())), preferred_element_type=f32)


def mm_split(a, b):
    a_high, b_high = a.astype(bf16), b.astype(bf16)
    a_low = (a - a_high.astype(f32)).astype(bf16)
    b_low = (b - b_high.astype(f32)).astype(bf16)
    return mm(a_high, b_high) + (mm(a_low, b_high) + mm(a_high, b_low))


def iotas(n):
    return (
        lax.broadcasted_iota(jnp.int32, (n, n), 0),
        lax.broadcasted_iota(jnp.int32, (n, n), 1),
    )


def call(kernel, outs, scratch, args, specs=None, flops=0, moved=0, into=VM):
    return pl.pallas_call(
        kernel,
        out_shape=outs,
        in_specs=specs or [VM] * len(args),
        out_specs=[into] * len(outs),
        scratch_shapes=scratch,
        cost_estimate=pl.CostEstimate(flops=flops, bytes_accessed=moved, transcendentals=0),
        compiler_params=pltpu.CompilerParams(vmem_limit_bytes=24 * 2**20),
    )(*args)


def order_kernel(dest_hbm, x_hbm, out_ref, dest_ref, x_ref, sems):
    first = pltpu.make_async_copy(dest_hbm, dest_ref, sems.at[0])
    second = pltpu.make_async_copy(x_hbm, x_ref, sems.at[1])
    first.start()
    second.start()
    row, _ = iotas(ROWS)
    first.wait()
    dest = dest_ref[...].astype(f32)
    across = jnp.broadcast_to(dest, (ROWS, ROWS))
    down = across.T
    rank = jnp.sum((down < across).astype(f32), axis=0, keepdims=True)
    pick = (rank == row.astype(f32)).astype(bf16)
    place = jnp.sum(pick.astype(f32) * (dest_ref[...] & (ROWS - 1)).astype(f32), axis=1, keepdims=True)
    place = jnp.broadcast_to(place, (ROWS, KEY)).astype(bf16)
    second.wait()
    moved = mm(pick, x_ref[...]).astype(bf16)
    for s in range(out_ref.shape[0]):
        for n in range(2):
            pair = slice(4 * s + 2 * n, 4 * s + 2 * n + 2)
            out_ref[s, :, n * WIDE : (n + 1) * WIDE] = moved[pair]
            out_ref[s, :, 2 * WIDE + n * 64 : 2 * WIDE + n * 64 + 64] = place[pair, n * 64 : n * 64 + 64]


def place_kernel(got_ref, weights_ref, upper_ref, lower_ref, low, high, places):
    for s in range(got_ref.shape[0]):
        pair = slice(2 * s, 2 * s + 2)
        low[pair, :] = got_ref[s, :, :WIDE]
        high[pair, :] = got_ref[s, :, WIDE : 2 * WIDE]
        places[pair, :] = got_ref[s, :, 2 * WIDE :]
    place = places[...].astype(f32).T
    slot = lax.broadcasted_iota(jnp.int32, (ROWS, HALF), 0).astype(f32)
    out = mm((place[:1] == slot).astype(bf16), low[...]) + mm((place[64:65] == slot).astype(bf16), high[...])
    upper_ref[...] = out[:HALF].astype(bf16)
    lower_ref[...] = out[HALF:].astype(bf16)


def silu(a):
    return a / (1.0 + jnp.exp(-a))


def doc_masks(doc_ref, t0):
    across = jnp.broadcast_to(doc_ref[...].astype(f32), (ROWS, ROWS))
    down = across.T
    same = across == down
    col = down[:, :1]
    carried = (col < t0).astype(f32)
    last = (col == col[ROWS - 1 : ROWS]).astype(f32)
    return same, carried, last


def first_row():
    return (lax.axis_index(SEQ) * ROWS).astype(f32)


def near_index():
    return lax.axis_index("zl") * 2 + lax.axis_index("c")


def project(pairs, wqk, wv, wb, acc, logit):
    for n, (x, off) in enumerate(pairs):
        start = pl.multiple_of(lax.rem(lax.axis_index("head") + off, 4) * WIDE, WIDE)
        part = mm_nt(x, wb[:, pl.ds(start, WIDE)])
        logit = part if logit is None else logit + part
        pairs[n] = (x, start)
    tiles = []
    for t in range(6):
        cols = slice(t * 256, t * 256 + 256)
        total = None if acc is None else acc[:, cols]
        for x, start in pairs:
            w = wqk[pl.ds(start, WIDE), cols] if t < 4 else wv[pl.ds(start, WIDE), t * 256 - 1024 : t * 256 - 768]
            part = mm(x, w)
            total = part if total is None else total + part
        tiles.append(total)
    return tiles, logit


def both(a, b):
    return jnp.concatenate([a[...], b[...]], axis=0)


def own_kernel(x0a, x0b, wqk, wv, wb, acc_out, logit_out):
    tiles, logit_out[...] = project([(both(x0a, x0b), 0)], wqk, wv, wb, None, None)
    for t in range(6):
        acc_out[:, t * 256 : t * 256 + 256] = tiles[t]


def beside_kernel(x1a, x1b, x3a, x3b, wqk, wv, wb, acc_in, logit_in, acc_out, logit_out):
    tiles, logit_out[...] = project([(both(x1a, x1b), 3), (both(x3a, x3b), 1)], wqk, wv, wb, acc_in, logit_in[...])
    for t in range(6):
        acc_out[:, t * 256 : t * 256 + 256] = tiles[t]


def terms_kernel(
    x2a, x2b, wqk, wv, wb, acc_in, logit_in, bias_ref, doc_ref,
    m0, m1, m2, m3, q_out, k_out, y_out,
    acc, maps,
):
    tiles, logit = project([(both(x2a, x2b), 2)], wqk, wv, wb, acc_in, logit_in[...])
    for t in range(6):
        acc[:, t * 256 : t * 256 + 256] = tiles[t]
    beta_all = beta_limit * (1.0 / (1.0 + jnp.exp(-(logit + bias_ref[...]))))

    same, carried, last = doc_masks(doc_ref, first_row())
    row, col = iotas(ROWS)
    strict = same & (row > col)
    r, c = iotas(HALF)
    eye = (r == c).astype(f32)
    by16 = (r >> 4) == (c >> 4)

    def level(s):
        return ((r >> (s + 1)) == (c >> (s + 1))) & ((r >> s) != (c >> s))

    q_out[...] = acc[:, :WIDE].astype(bf16)
    rhs, cross, low = [], [], []
    for h in range(HEADS):
        def raw(base):
            piece = acc[:, base + h * KEY : base + (h + 1) * KEY]
            return silu(piece.astype(bf16).astype(f32))

        k = raw(WIDE)
        k = k / jnp.sqrt(jnp.sum(k * k, axis=-1, keepdims=True) + key_eps)
        kb = k.astype(bf16)
        k_out[h] = kb
        v = raw(2 * WIDE)
        beta = beta_all[:, h : h + 1]
        rhs.append(jnp.concatenate([(beta * carried) * k, beta * v], axis=1).astype(bf16))
        top, bot = kb[:HALF], kb[HALF:]
        b_top, b_bot = beta[:HALF], beta[HALF:]
        low.append(jnp.where(strict[:HALF, :HALF], b_top * mm_nt(top, top), 0.0))
        low.append(jnp.where(strict[HALF:, HALF:], b_bot * mm_nt(bot, bot), 0.0))
        cross.append(jnp.where(strict[HALF:, :HALF], b_bot * mm_nt(bot, top), 0.0).astype(bf16))

    n1 = [jnp.where(by16, m, 0.0) for m in low]
    inv = [eye - m for m in n1]
    power = [m.astype(bf16) for m in n1]
    for _ in range(3):
        power = [mm(m, m).astype(bf16) for m in power]
        inv = [x + mm(x.astype(bf16), m) for x, m in zip(inv, power)]
    for s in (4, 5, 6):
        mask = level(s)
        xb = [x.astype(bf16) for x in inv]
        mid = [mm(jnp.where(mask, m, 0.0).astype(bf16), x).astype(bf16) for m, x in zip(low, xb)]
        inv = [x - mm(y, m) for x, y, m in zip(inv, xb, mid)]
    inv = [x.astype(bf16) for x in inv]
    full_top = [mm(inv[2 * h], rhs[h][:HALF]) for h in range(HEADS)]
    y_top = [y.astype(bf16) for y in full_top]
    y_mid = [(rhs[h][HALF:].astype(f32) - mm(cross[h], y_top[h])).astype(bf16) for h in range(HEADS)]
    full_bot = [mm(inv[2 * h + 1], y_mid[h]) for h in range(HEADS)]
    y_bot = [y.astype(bf16) for y in full_bot]
    reset = jnp.where(carried[ROWS - 1 : ROWS] > 0, 0.0, 1.0) * eye
    reset = jnp.concatenate([reset, jnp.zeros((KEY, KEY), f32)], axis=1)
    for h in range(HEADS):
        y_out[h, :HALF] = full_top[h]
        y_out[h, HALF:] = full_bot[h]
        last_keys = (k_out[h].astype(f32) * last).astype(bf16)
        total = mm_tn(last_keys[:HALF], y_top[h]) + mm_tn(last_keys[HALF:], y_bot[h])
        maps[h] = (total + reset).astype(bf16)
    near = near_index()
    for n, ref in enumerate((m0, m1, m2, m3)):
        ref[...] = maps[near ^ n]


def read_kernel(q_ref, k_ref, y_ref, doc_ref, local_out, query_out):
    same, carried, _ = doc_masks(doc_ref, first_row())
    row, col = iotas(ROWS)
    mask = same & (row >= col)
    for h in range(HEADS):
        q = silu(q_ref[:, h * KEY : (h + 1) * KEY].astype(f32))
        scores = jnp.where(mask, mm_nt(q.astype(bf16), k_ref[h]), 0.0)
        terms = mm_split(scores, y_ref[h])
        query_out[h] = (q * carried - terms[:, :KEY]).astype(bf16)
        local_out[h] = terms[:, KEY:]


def after(first, then):
    firm = first.astype(bf16)
    return firm.astype(f32) + then.astype(f32) - mm(then[:, :KEY].astype(bf16), firm)


def chosen(which, options):
    out = options[0]
    for n in range(1, len(options)):
        out = jnp.where(which == n, options[n], out)
    return out


def in_order(me, refs, slots):
    for n, ref in enumerate(refs):
        slots[me ^ n] = ref[...]


def near_kernel(a, b, c, d, total, prefix, slots):
    in_order(near_index(), (a, b, c, d), slots)
    run = slots[0]
    prefix[0] = run
    for n in (1, 2, 3):
        run = after(run, slots[n]).astype(bf16)
        if n < 3:
            prefix[n] = run
    total[...] = run


def pair_kernel(mine, other, total, first_out):
    upper = (lax.axis_index("zh") & 1) == 1
    first = jnp.where(upper, other[...], mine[...])
    total[...] = after(first, jnp.where(upper, mine[...], other[...])).astype(bf16)
    first_out[...] = first


def far_kernel(mine, other, first, total, prefix):
    me = lax.axis_index("zh")
    upper = me >= 2
    low = jnp.where(upper, other[...], mine[...])
    total[...] = after(low, jnp.where(upper, mine[...], other[...])).astype(bf16)
    low = low.astype(f32)
    later = after(low, first[...])
    prefix[...] = chosen(me, [jnp.zeros_like(low), first[...].astype(f32), low, later]).astype(bf16)


def apply_map(step, state):
    firm = state.astype(bf16)
    return firm.astype(f32) - mm(step[:, :KEY], firm) + step[:, KEY:].astype(f32)


def plane_kernel(mine, other, near, far, carried_out, first_out, steps):
    upper = (lax.axis_index("y") & 1) == 1
    first = jnp.where(upper, other[...], mine[...])
    second = jnp.where(upper, mine[...], other[...])
    carried_out[...] = apply_map(second, first[:, KEY:]).astype(bf16)
    first_out[...] = first
    steps[0] = far[...]
    for n in range(3):
        steps[n + 1] = after(far[...], near[n]).astype(bf16)


def state_kernel(came, first, steps, s0, s1, s2, s3, states):
    me = lax.axis_index("y")
    state = jnp.where(me >= 2, came[...].astype(f32), 0.0)
    state = jnp.where((me & 1) == 1, apply_map(first[...], state), state).astype(bf16)
    for n in range(4):
        states[n] = apply_map(steps[n], state).astype(bf16)
    place = near_index()
    for n, ref in enumerate((s0, s1, s2, s3)):
        ref[...] = states[place ^ n]


def out_kernel(a, b, c, d, local_ref, query_ref, gain_ref, out_hbm, slots, done, sems):
    in_order(near_index(), (a, b, c, d), slots)
    copies = []
    for h in range(HEADS):
        out = local_ref[h] + mm(query_ref[h], slots[h])
        mean = jnp.mean(out * out, axis=-1, keepdims=True)
        done[h] = (out * lax.rsqrt(mean + rms_eps) * gain_ref[...]).astype(bf16)
        copies.append(pltpu.make_async_copy(done.at[h], out_hbm.at[:, pl.ds(h * KEY, KEY)], sems.at[h]))
        copies[h].start()
    for copy in copies:
        copy.wait()


def turned(x, axis, by):
    return lax.ppermute(x, axis, [(i, (i + by) % 4) for i in range(4)])


def swapped(x, axis, by):
    return lax.ppermute(x, axis, [(i, i ^ by) for i in range(4)])


def local(x_loader, dest, doc_start, w_qk, w_v, w_beta, beta_bias, out_gain):
    shape = jax.ShapeDtypeStruct
    vmem = pltpu.VMEM
    doc = doc_start.reshape(1, ROWS)
    peers = lax.axis_size(SEQ)
    in_hbm = pl.BlockSpec(memory_space=pltpu.HBM)
    (sent,) = call(
        order_kernel,
        [shape((peers, 2, 2 * WIDE + KEY), bf16)],
        [vmem((1, ROWS), jnp.int32), vmem((ROWS, WIDE), bf16), pltpu.SemaphoreType.DMA((2,))],
        [pltpu.with_memory_space_constraint(x, pltpu.HBM) for x in (dest.reshape(1, ROWS), x_loader)],
        specs=[in_hbm, in_hbm],
    )
    got = lax.all_to_all(sent, SEQ, split_axis=0, concat_axis=0, tiled=True)
    flat_qk = w_qk.reshape(w_qk.shape[0], -1)
    upper, lower = call(place_kernel, [shape((HALF, WIDE), bf16)] * 2, [vmem((HALF, WIDE), bf16), vmem((HALF, WIDE), bf16), vmem((HALF, KEY), bf16)], (got, pltpu.with_memory_space_constraint(flat_qk, pltpu.HBM)), specs=[VM, in_hbm])
    left_upper = turned(upper, "head", 1)
    right_lower = turned(lower, "head", 3)
    left_lower = turned(lower, "head", 1)
    right_upper = turned(upper, "head", 3)
    across_upper = turned(left_upper, "head", 1)
    across_lower = turned(right_lower, "head", 3)
    weights = (flat_qk, w_v, w_beta.T)
    sums = [shape((ROWS, 3 * WIDE), f32), shape((ROWS, HEADS), f32)]
    part = call(own_kernel, sums, [], (upper, lower, *weights), flops=4 * 10**8, moved=3 * 10**6)
    part = call(
        beside_kernel, sums, [], (left_upper, left_lower, right_upper, right_lower, *weights, *part), flops=8 * 10**8, moved=6 * 10**6
    )
    one_map = shape((KEY, 2 * KEY), bf16)
    m0, m1, m2, m3, q, k, y = call(
        terms_kernel,
        [one_map] * 4
        + [shape((ROWS, WIDE), bf16), shape((HEADS, ROWS, KEY), bf16), shape((HEADS, ROWS, 2 * KEY), f32)],
        [vmem((ROWS, 3 * WIDE), f32), vmem((HEADS, KEY, 2 * KEY), bf16)],
        (across_upper, across_lower, *weights, *part, beta_bias.reshape(1, HEADS), doc),
        flops=2 * 10**9,
        moved=4 * 10**6,
    )
    slots = [vmem((4, KEY, 2 * KEY), bf16)]
    n3, n2, n1 = (swapped(m, NEAR, n) for m, n in ((m3, 3), (m2, 2), (m1, 1)))
    near = (m0, n1, n2, n3)
    local_out, query = call(
        read_kernel,
        [shape((HEADS, ROWS, KEY), f32), shape((HEADS, ROWS, KEY), bf16)],
        [],
        (q, k, y, doc),
        flops=10**9,
        moved=2 * 10**6,
    )
    group, prefix = call(near_kernel, [one_map, shape((3, KEY, 2 * KEY), bf16)], slots, near)
    half_plane, first = call(pair_kernel, [one_map, one_map], [], (group, swapped(group, "zh", 1)))
    plane, far_prefix = call(
        far_kernel, [one_map, one_map], [], (half_plane, swapped(half_plane, "zh", 3), first)
    )
    carried, first, steps = call(
        plane_kernel,
        [shape((KEY, KEY), bf16), one_map, shape((4, KEY, 2 * KEY), bf16)],
        [],
        (plane, swapped(plane, "y", 1), prefix, far_prefix),
    )
    s0, s1, s2, s3 = call(
        state_kernel,
        [shape((KEY, KEY), bf16)] * 4,
        [vmem((4, KEY, KEY), bf16)],
        (swapped(carried, "y", 3), first, steps),
    )
    t3, t2, t1 = (swapped(m, NEAR, n) for m, n in ((s3, 3), (s2, 2), (s1, 1)))
    states = (s0, t1, t2, t3)
    (out,) = call(
        out_kernel,
        [shape((ROWS, WIDE), bf16)],
        [vmem((4, KEY, KEY), bf16), vmem((HEADS, ROWS, KEY), bf16), pltpu.SemaphoreType.DMA((HEADS,))],
        (*states, local_out, query, out_gain.reshape(1, KEY)),
        into=ANY,
    )
    return out


def solution(mesh):
    torus = Mesh(mesh.devices.reshape(4, 4, 2, 2, mesh.shape["head"]), (*SEQ, "head"))
    return jax.shard_map(
        local,
        mesh=torus,
        in_specs=(
            P(SEQ, "head"),
            P(SEQ),
            P(SEQ),
            P(None, None, "head"),
            P(None, "head"),
            P(None, "head"),
            P("head"),
            P(),
        ),
        out_specs=P(SEQ, "head"),
        check_vma=False,
    )
```

```python
import jax
import jax.numpy as jnp
from jax import lax
from jax.experimental import pallas as pl
from jax.experimental.pallas import tpu as pltpu
from jax.sharding import Mesh
from jax.sharding import PartitionSpec as P


SEQ = ("y", "zh", "zl", "c")
NEAR = ("zl", "c")
ROWS = 256
HALF = 128
WIDE = 512
HEADS = 4
KEY = 128
beta_limit = 0.1
key_eps = 1e-06
rms_eps = 1e-05
bf16 = jnp.bfloat16
f32 = jnp.float32
ANY = pl.BlockSpec(memory_space=pl.ANY)
VM = pl.BlockSpec(memory_space=pltpu.VMEM)


def mm(a, b):
    return lax.dot_general(a, b, (((1,), (0,)), ((), ())), preferred_element_type=f32)


def mm_nt(a, b):
    return lax.dot_general(a, b, (((1,), (1,)), ((), ())), preferred_element_type=f32)


def mm_tn(a, b):
    return lax.dot_general(a, b, (((0,), (0,)), ((), ())), preferred_element_type=f32)


def mm_split(a, b):
    a_high, b_high = a.astype(bf16), b.astype(bf16)
    a_low = (a - a_high.astype(f32)).astype(bf16)
    b_low = (b - b_high.astype(f32)).astype(bf16)
    return mm(a_high, b_high) + (mm(a_low, b_high) + mm(a_high, b_low))


def iotas(n):
    return (
        lax.broadcasted_iota(jnp.int32, (n, n), 0),
        lax.broadcasted_iota(jnp.int32, (n, n), 1),
    )


def call(kernel, outs, scratch, args, specs=None, flops=0, moved=0, into=VM):
    return pl.pallas_call(
        kernel,
        out_shape=outs,
        in_specs=specs or [VM] * len(args),
        out_specs=[into] * len(outs),
        scratch_shapes=scratch,
        cost_estimate=pl.CostEstimate(flops=flops, bytes_accessed=moved, transcendentals=0),
        compiler_params=pltpu.CompilerParams(vmem_limit_bytes=24 * 2**20),
    )(*args)


def order_kernel(dest_hbm, x_hbm, out_ref, dest_ref, x_ref, sems):
    first = pltpu.make_async_copy(dest_hbm, dest_ref, sems.at[0])
    second = pltpu.make_async_copy(x_hbm, x_ref, sems.at[1])
    first.start()
    second.start()
    row, _ = iotas(ROWS)
    first.wait()
    dest = dest_ref[...].astype(f32)
    across = jnp.broadcast_to(dest, (ROWS, ROWS))
    down = across.T
    rank = jnp.sum((down < across).astype(f32), axis=0, keepdims=True)
    pick = (rank == row.astype(f32)).astype(bf16)
    place = jnp.sum(pick.astype(f32) * (dest_ref[...] & (ROWS - 1)).astype(f32), axis=1, keepdims=True)
    place = jnp.broadcast_to(place, (ROWS, KEY)).astype(bf16)
    second.wait()
    moved = mm(pick, x_ref[...]).astype(bf16)
    for s in range(out_ref.shape[0]):
        for n in range(2):
            pair = slice(4 * s + 2 * n, 4 * s + 2 * n + 2)
            out_ref[s, :, n * WIDE : (n + 1) * WIDE] = moved[pair]
            out_ref[s, :, 2 * WIDE + n * 64 : 2 * WIDE + n * 64 + 64] = place[pair, n * 64 : n * 64 + 64]


def place_kernel(got_ref, weights_ref, upper_ref, lower_ref, low, high, places):
    for s in range(got_ref.shape[0]):
        pair = slice(2 * s, 2 * s + 2)
        low[pair, :] = got_ref[s, :, :WIDE]
        high[pair, :] = got_ref[s, :, WIDE : 2 * WIDE]
        places[pair, :] = got_ref[s, :, 2 * WIDE :]
    place = places[...].astype(f32).T
    slot = lax.broadcasted_iota(jnp.int32, (ROWS, HALF), 0).astype(f32)
    out = mm((place[:1] == slot).astype(bf16), low[...]) + mm((place[64:65] == slot).astype(bf16), high[...])
    upper_ref[...] = out[:HALF].astype(bf16)
    lower_ref[...] = out[HALF:].astype(bf16)


def silu(a):
    return a / (1.0 + jnp.exp(-a))


def doc_masks(doc_ref, t0):
    across = jnp.broadcast_to(doc_ref[...].astype(f32), (ROWS, ROWS))
    down = across.T
    same = across == down
    col = down[:, :1]
    carried = (col < t0).astype(f32)
    last = (col == col[ROWS - 1 : ROWS]).astype(f32)
    return same, carried, last


def first_row():
    return (lax.axis_index(SEQ) * ROWS).astype(f32)


def near_index():
    return lax.axis_index("zl") * 2 + lax.axis_index("c")


def project(pairs, wqk, wv, wb, acc, logit):
    for n, (x, off) in enumerate(pairs):
        start = pl.multiple_of(lax.rem(lax.axis_index("head") + off, 4) * WIDE, WIDE)
        part = mm_nt(x, wb[:, pl.ds(start, WIDE)])
        logit = part if logit is None else logit + part
        pairs[n] = (x, start)
    tiles = []
    for t in range(6):
        cols = slice(t * 256, t * 256 + 256)
        total = None if acc is None else acc[:, cols]
        for x, start in pairs:
            w = wqk[pl.ds(start, WIDE), cols] if t < 4 else wv[pl.ds(start, WIDE), t * 256 - 1024 : t * 256 - 768]
            part = mm(x, w)
            total = part if total is None else total + part
        tiles.append(total)
    return tiles, logit


def both(a, b):
    return jnp.concatenate([a[...], b[...]], axis=0)


def own_kernel(x0a, x0b, wqk, wv, wb, acc_out, logit_out):
    tiles, logit_out[...] = project([(both(x0a, x0b), 0)], wqk, wv, wb, None, None)
    for t in range(6):
        acc_out[:, t * 256 : t * 256 + 256] = tiles[t]


def beside_kernel(x1a, x1b, x3a, x3b, wqk, wv, wb, acc_in, logit_in, acc_out, logit_out):
    tiles, logit_out[...] = project([(both(x1a, x1b), 3), (both(x3a, x3b), 1)], wqk, wv, wb, acc_in, logit_in[...])
    for t in range(6):
        acc_out[:, t * 256 : t * 256 + 256] = tiles[t]


def terms_kernel(
    x2a, x2b, wqk, wv, wb, acc_in, logit_in, bias_ref, doc_ref,
    m0, m1, m2, m3, q_out, k_out, y_out,
    acc, maps,
):
    tiles, logit = project([(both(x2a, x2b), 2)], wqk, wv, wb, acc_in, logit_in[...])
    for t in range(6):
        acc[:, t * 256 : t * 256 + 256] = tiles[t]
    beta_all = beta_limit * (1.0 / (1.0 + jnp.exp(-(logit + bias_ref[...]))))

    same, carried, last = doc_masks(doc_ref, first_row())
    row, col = iotas(ROWS)
    strict = same & (row > col)
    r, c = iotas(HALF)
    eye = (r == c).astype(f32)
    by16 = (r >> 4) == (c >> 4)

    def level(s):
        return ((r >> (s + 1)) == (c >> (s + 1))) & ((r >> s) != (c >> s))

    q_out[...] = acc[:, :WIDE].astype(bf16)
    rhs, cross, low = [], [], []
    for h in range(HEADS):
        def raw(base):
            piece = acc[:, base + h * KEY : base + (h + 1) * KEY]
            return silu(piece.astype(bf16).astype(f32))

        k = raw(WIDE)
        k = k / jnp.sqrt(jnp.sum(k * k, axis=-1, keepdims=True) + key_eps)
        kb = k.astype(bf16)
        k_out[h] = kb
        v = raw(2 * WIDE)
        beta = beta_all[:, h : h + 1]
        rhs.append(jnp.concatenate([(beta * carried) * k, beta * v], axis=1).astype(bf16))
        top, bot = kb[:HALF], kb[HALF:]
        b_top, b_bot = beta[:HALF], beta[HALF:]
        low.append(jnp.where(strict[:HALF, :HALF], b_top * mm_nt(top, top), 0.0))
        low.append(jnp.where(strict[HALF:, HALF:], b_bot * mm_nt(bot, bot), 0.0))
        cross.append(jnp.where(strict[HALF:, :HALF], b_bot * mm_nt(bot, top), 0.0).astype(bf16))

    n1 = [jnp.where(by16, m, 0.0) for m in low]
    inv = [eye - m for m in n1]
    power = [m.astype(bf16) for m in n1]
    for _ in range(3):
        power = [mm(m, m).astype(bf16) for m in power]
        inv = [x + mm(x.astype(bf16), m) for x, m in zip(inv, power)]
    for s in (4, 5, 6):
        mask = level(s)
        xb = [x.astype(bf16) for x in inv]
        mid = [mm(jnp.where(mask, m, 0.0).astype(bf16), x).astype(bf16) for m, x in zip(low, xb)]
        inv = [x - mm(y, m) for x, y, m in zip(inv, xb, mid)]
    inv = [x.astype(bf16) for x in inv]
    full_top = [mm(inv[2 * h], rhs[h][:HALF]) for h in range(HEADS)]
    y_top = [y.astype(bf16) for y in full_top]
    y_mid = [(rhs[h][HALF:].astype(f32) - mm(cross[h], y_top[h])).astype(bf16) for h in range(HEADS)]
    full_bot = [mm(inv[2 * h + 1], y_mid[h]) for h in range(HEADS)]
    y_bot = [y.astype(bf16) for y in full_bot]
    reset = jnp.where(carried[ROWS - 1 : ROWS] > 0, 0.0, 1.0) * eye
    reset = jnp.concatenate([reset, jnp.zeros((KEY, KEY), f32)], axis=1)
    for h in range(HEADS):
        y_out[h, :HALF] = full_top[h]
        y_out[h, HALF:] = full_bot[h]
        last_keys = (k_out[h].astype(f32) * last).astype(bf16)
        total = mm_tn(last_keys[:HALF], y_top[h]) + mm_tn(last_keys[HALF:], y_bot[h])
        maps[h] = (total + reset).astype(bf16)
    near = near_index()
    for n, ref in enumerate((m0, m1, m2, m3)):
        ref[...] = maps[near ^ n]


def read_kernel(q_ref, k_ref, y_ref, doc_ref, local_out, query_out):
    same, carried, _ = doc_masks(doc_ref, first_row())
    row, col = iotas(ROWS)
    mask = same & (row >= col)
    for h in range(HEADS):
        q = silu(q_ref[:, h * KEY : (h + 1) * KEY].astype(f32))
        scores = jnp.where(mask, mm_nt(q.astype(bf16), k_ref[h]), 0.0)
        terms = mm_split(scores, y_ref[h])
        query_out[h] = (q * carried - terms[:, :KEY]).astype(bf16)
        local_out[h] = terms[:, KEY:]


def after(first, then):
    firm = first.astype(bf16)
    return firm.astype(f32) + then.astype(f32) - mm(then[:, :KEY].astype(bf16), firm)


def chosen(which, options):
    out = options[0]
    for n in range(1, len(options)):
        out = jnp.where(which == n, options[n], out)
    return out


def in_order(me, refs, slots):
    for n, ref in enumerate(refs):
        slots[me ^ n] = ref[...]


def near_kernel(a, b, c, d, total, prefix, slots):
    in_order(near_index(), (a, b, c, d), slots)
    low = after(slots[0], slots[1]).astype(bf16)
    high = after(slots[2], slots[3])
    total[...] = after(low, high).astype(bf16)
    prefix[0] = slots[0]
    prefix[1] = low
    prefix[2] = after(low, slots[2]).astype(bf16)


def pair_kernel(mine, other, total, first_out):
    upper = (lax.axis_index("zh") & 1) == 1
    first = jnp.where(upper, other[...], mine[...])
    total[...] = after(first, jnp.where(upper, mine[...], other[...])).astype(bf16)
    first_out[...] = first


def far_kernel(mine, other, first, total, prefix):
    me = lax.axis_index("zh")
    upper = me >= 2
    low = jnp.where(upper, other[...], mine[...])
    total[...] = after(low, jnp.where(upper, mine[...], other[...])).astype(bf16)
    low = low.astype(f32)
    later = after(low, first[...])
    prefix[...] = chosen(me, [jnp.zeros_like(low), first[...].astype(f32), low, later]).astype(bf16)


def apply_map(step, state):
    firm = state.astype(bf16)
    return firm.astype(f32) - mm(step[:, :KEY], firm) + step[:, KEY:].astype(f32)


def plane_kernel(mine, other, near, far, carried_out, first_out, steps):
    upper = (lax.axis_index("y") & 1) == 1
    first = jnp.where(upper, other[...], mine[...])
    second = jnp.where(upper, mine[...], other[...])
    carried_out[...] = apply_map(second, first[:, KEY:]).astype(bf16)
    first_out[...] = first
    steps[0] = far[...]
    for n in range(3):
        steps[n + 1] = after(far[...], near[n]).astype(bf16)


def state_kernel(came, first, steps, s0, s1, s2, s3, states):
    me = lax.axis_index("y")
    state = jnp.where(me >= 2, came[...].astype(f32), 0.0)
    state = jnp.where((me & 1) == 1, apply_map(first[...], state), state).astype(bf16)
    for n in range(4):
        states[n] = apply_map(steps[n], state).astype(bf16)
    place = near_index()
    for n, ref in enumerate((s0, s1, s2, s3)):
        ref[...] = states[place ^ n]


def out_kernel(a, b, c, d, local_ref, query_ref, gain_ref, out_hbm, slots, done, sems):
    in_order(near_index(), (a, b, c, d), slots)
    copies = []
    for h in range(HEADS):
        out = local_ref[h] + mm(query_ref[h], slots[h])
        mean = jnp.mean(out * out, axis=-1, keepdims=True)
        done[h] = (out * lax.rsqrt(mean + rms_eps) * gain_ref[...]).astype(bf16)
        copies.append(pltpu.make_async_copy(done.at[h], out_hbm.at[:, pl.ds(h * KEY, KEY)], sems.at[h]))
        copies[h].start()
    for copy in copies:
        copy.wait()


def turned(x, axis, by):
    return lax.ppermute(x, axis, [(i, (i + by) % 4) for i in range(4)])


def swapped(x, axis, by):
    return lax.ppermute(x, axis, [(i, i ^ by) for i in range(4)])


def local(x_loader, dest, doc_start, w_qk, w_v, w_beta, beta_bias, out_gain):
    shape = jax.ShapeDtypeStruct
    vmem = pltpu.VMEM
    doc = doc_start.reshape(1, ROWS)
    peers = lax.axis_size(SEQ)
    in_hbm = pl.BlockSpec(memory_space=pltpu.HBM)
    (sent,) = call(
        order_kernel,
        [shape((peers, 2, 2 * WIDE + KEY), bf16)],
        [vmem((1, ROWS), jnp.int32), vmem((ROWS, WIDE), bf16), pltpu.SemaphoreType.DMA((2,))],
        [pltpu.with_memory_space_constraint(x, pltpu.HBM) for x in (dest.reshape(1, ROWS), x_loader)],
        specs=[in_hbm, in_hbm],
    )
    got = lax.all_to_all(sent, SEQ, split_axis=0, concat_axis=0, tiled=True)
    flat_qk = w_qk.reshape(w_qk.shape[0], -1)
    upper, lower = call(place_kernel, [shape((HALF, WIDE), bf16)] * 2, [vmem((HALF, WIDE), bf16), vmem((HALF, WIDE), bf16), vmem((HALF, KEY), bf16)], (got, pltpu.with_memory_space_constraint(flat_qk, pltpu.HBM)), specs=[VM, in_hbm])
    left_upper = turned(upper, "head", 1)
    right_lower = turned(lower, "head", 3)
    left_lower = turned(lower, "head", 1)
    right_upper = turned(upper, "head", 3)
    across_upper = turned(left_upper, "head", 1)
    across_lower = turned(right_lower, "head", 3)
    weights = (flat_qk, w_v, w_beta.T)
    sums = [shape((ROWS, 3 * WIDE), f32), shape((ROWS, HEADS), f32)]
    part = call(own_kernel, sums, [], (upper, lower, *weights), flops=4 * 10**8, moved=3 * 10**6)
    part = call(
        beside_kernel, sums, [], (left_upper, left_lower, right_upper, right_lower, *weights, *part), flops=8 * 10**8, moved=6 * 10**6
    )
    one_map = shape((KEY, 2 * KEY), bf16)
    m0, m1, m2, m3, q, k, y = call(
        terms_kernel,
        [one_map] * 4
        + [shape((ROWS, WIDE), bf16), shape((HEADS, ROWS, KEY), bf16), shape((HEADS, ROWS, 2 * KEY), f32)],
        [vmem((ROWS, 3 * WIDE), f32), vmem((HEADS, KEY, 2 * KEY), bf16)],
        (across_upper, across_lower, *weights, *part, beta_bias.reshape(1, HEADS), doc),
        flops=2 * 10**9,
        moved=4 * 10**6,
    )
    slots = [vmem((4, KEY, 2 * KEY), bf16)]
    n3, n2, n1 = (swapped(m, NEAR, n) for m, n in ((m3, 3), (m2, 2), (m1, 1)))
    near = (m0, n1, n2, n3)
    local_out, query = call(
        read_kernel,
        [shape((HEADS, ROWS, KEY), f32), shape((HEADS, ROWS, KEY), bf16)],
        [],
        (q, k, y, doc),
        flops=10**9,
        moved=2 * 10**6,
    )
    group, prefix = call(near_kernel, [one_map, shape((3, KEY, 2 * KEY), bf16)], slots, near)
    half_plane, first = call(pair_kernel, [one_map, one_map], [], (group, swapped(group, "zh", 1)))
    plane, far_prefix = call(
        far_kernel, [one_map, one_map], [], (half_plane, swapped(half_plane, "zh", 3), first)
    )
    carried, first, steps = call(
        plane_kernel,
        [shape((KEY, KEY), bf16), one_map, shape((4, KEY, 2 * KEY), bf16)],
        [],
        (plane, swapped(plane, "y", 1), prefix, far_prefix),
    )
    s0, s1, s2, s3 = call(
        state_kernel,
        [shape((KEY, KEY), bf16)] * 4,
        [vmem((4, KEY, KEY), bf16)],
        (swapped(carried, "y", 3), first, steps),
    )
    t3, t2, t1 = (swapped(m, NEAR, n) for m, n in ((s3, 3), (s2, 2), (s1, 1)))
    states = (s0, t1, t2, t3)
    (out,) = call(
        out_kernel,
        [shape((ROWS, WIDE), bf16)],
        [vmem((4, KEY, KEY), bf16), vmem((HEADS, ROWS, KEY), bf16), pltpu.SemaphoreType.DMA((HEADS,))],
        (*states, local_out, query, out_gain.reshape(1, KEY)),
        into=ANY,
    )
    return out


def solution(mesh):
    torus = Mesh(mesh.devices.reshape(4, 4, 2, 2, mesh.shape["head"]), (*SEQ, "head"))
    return jax.shard_map(
        local,
        mesh=torus,
        in_specs=(
            P(SEQ, "head"),
            P(SEQ),
            P(SEQ),
            P(None, None, "head"),
            P(None, "head"),
            P(None, "head"),
            P("head"),
            P(),
        ),
        out_specs=P(SEQ, "head"),
        check_vma=False,
    )
```
